32 devices in a mesh: run: 2 (over y), tile: 16 (over z, x, core).
Axes of the slice: x: 2, y: 2, z: 4, core: 2. Of those that a mesh axis runs over, the one named last changes fastest.
Arguments:
- clip: bfloat16 [32, 64, 128, 128], P(('run', 'tile')), parts along dimension 0, may hold values from -6 to 6
- w_space: bfloat16 [9, 64, 64], replicated, may hold values from -0.25 to 0.25
- w_time: bfloat16 [2, 3, 64, 64], replicated, may hold values from -0.4375 to 0.4375
- cotangent: bfloat16 [32, 64, 128, 128], P('run', None, 'tile'), parts along dimension 0, may hold values from -6 to 6
Outputs:
- output: bfloat16 [32, 64, 128, 128], P('run', None, 'tile'), parts along dimension 0
- grad_clip: bfloat16 [32, 64, 128, 128], P(('run', 'tile')), parts along dimension 0
- grad_space: float32 [18, 64, 64], P('run'), parts along dimension 0
- grad_time: float32 [4, 3, 64, 64], P('run'), parts along dimension 0
The draws below stay inside these ranges and needn't reach their ends.
There are 2 independent parts, one for each index of `run`. The reference program is written for one: setup_inputs(seed, part) draws one part's arguments, and reference() takes and returns one part's arrays. A program takes and returns all parts, laid end to end along the dimension named above; an argument that names none is the same for every part. Nothing has to cross between parts.
All inputs are finite; a program needn't handle non-finite values.
Results may differ from the reference program's by a relative error of at most 0.0062.
Values may be sent and summed in bfloat16 or wider, within the bound.
No kernel may reach another device: no remote copies, remote signals or barrier semaphores. Data moves between devices by JAX's collectives and lax.ppermute only.
A program may use at most 128 MiB of HBM per device.

```python
import math
import jax
import jax.numpy as jnp
from jax import lax

C = 64
H = 128
W = 128
LAYERS = 2
FRAMES = 16
N_TILE = 16


def block_scale(rng, shape, split, smallest, top_value):
    factor_of = 1.0
    for axis_at, blocks in split:
        draws = jax.random.uniform(jax.random.fold_in(jax.random.fold_in(rng, 6), axis_at), (blocks,), jnp.float32, smallest / len(split), top_value / len(split))
        factor_of = factor_of * jnp.repeat(jnp.exp(draws), shape[axis_at] // blocks).reshape((-1,) + (1,) * (len(shape) - 1 - axis_at))
    return factor_of


def gaussian(rng, shape, scale, most, shards=(), kind=jnp.bfloat16):
    level = block_scale(rng, shape, shards, -0.22, 0.18) if shards else 1.0
    array = jax.random.normal(rng, shape, jnp.float32) * scale * level
    return jnp.minimum(jnp.maximum(array, -most), most).astype(kind)


def setup_inputs(seed: int = 0, part: int = 0) -> dict:
    keys = jax.random.split(jax.random.key(seed), 5)
    part_keys = jax.random.split(jax.random.fold_in(keys[4], part), 5)
    return {
        "clip": gaussian(part_keys[0], (FRAMES, C, H, W), 1.0, 6.0, ((0, 16),)),
        "w_space": gaussian(keys[1], (9, C, C), (9 * C) ** -0.5, 0.25),
        "w_time": gaussian(keys[2], (LAYERS, 3, C, C), (3 * C) ** -0.5, 0.4375),
        "cotangent": gaussian(part_keys[3], (FRAMES, C, H, W), 1.0, 6.0, ((2, 16),)),
    }


def silu_slope(value):
    sigma = jax.nn.sigmoid(value)
    return sigma * (1.0 + value * (1.0 - sigma))

def space_conv(frame, w_space):
    row_count, column_count = (frame.shape[1], frame.shape[2])
    padded = jnp.pad(frame.astype(jnp.float32), ((0, 0), (1, 1), (1, 1)))
    weights = w_space.astype(jnp.float32)
    total = jnp.zeros((w_space.shape[1], row_count, column_count), jnp.float32)
    for tap_row in range(3):
        for tap_col in range(3):
            window = padded[:, tap_row:tap_row + row_count, tap_col:tap_col + column_count]
            total = total + jnp.einsum('oc,chw->ohw', weights[tap_row * 3 + tap_col], window)
    return total

def space_back(frame, slope_grad, w_space):
    row_count, column_count = (frame.shape[1], frame.shape[2])
    padded_x = jnp.pad(frame.astype(jnp.float32), ((0, 0), (1, 1), (1, 1)))
    grad_f = slope_grad.astype(jnp.float32)
    padded_g = jnp.pad(grad_f, ((0, 0), (1, 1), (1, 1)))
    weights = w_space.astype(jnp.float32)
    grad_frame = jnp.zeros(frame.shape, jnp.float32)
    kernel_terms = []
    for tap_row in range(3):
        for tap_col in range(3):
            tap = tap_row * 3 + tap_col
            shifted_g = padded_g[:, 2 - tap_row:2 - tap_row + row_count, 2 - tap_col:2 - tap_col + column_count]
            grad_frame = grad_frame + jnp.einsum('oc,ohw->chw', weights[tap], shifted_g)
            window = padded_x[:, tap_row:tap_row + row_count, tap_col:tap_col + column_count]
            kernel_terms.append(jnp.einsum('ohw,chw->oc', grad_f, window))
    return (grad_frame.astype(jnp.bfloat16), jnp.stack(kernel_terms))

def causal_mix(states_in, weights, spacing):
    frames = states_in.shape[0]
    values = states_in.astype(jnp.float32)
    wf = weights.astype(jnp.float32)
    total = jnp.einsum('oc,tcp->top', wf[0], values)
    for tap in (1, 2):
        amount = tap * spacing
        shifted = jnp.pad(values, ((amount, 0), (0, 0), (0, 0)))[:frames]
        total = total + jnp.einsum('oc,tcp->top', wf[tap], shifted)
    return total

def time_block(u_block, g_block, w_time):
    frames = u_block.shape[0]
    layer_count = w_time.shape[0]
    states = [u_block]
    for layer in range(layer_count):
        mixed = causal_mix(states[-1], w_time[layer], 2 ** layer)
        states.append((states[-1].astype(jnp.float32) + jax.nn.silu(mixed)).astype(jnp.bfloat16))
    error = g_block.astype(jnp.float32)
    grads = [None] * layer_count
    for layer in reversed(range(layer_count)):
        spacing = 2 ** layer
        mixed = causal_mix(states[layer], w_time[layer], spacing)
        gated = (error * silu_slope(mixed)).astype(jnp.bfloat16).astype(jnp.float32)
        earlier_all = states[layer].astype(jnp.float32)
        wf = w_time[layer].astype(jnp.float32)
        taps = []
        for tap in range(3):
            amount = tap * spacing
            earlier = jnp.pad(earlier_all, ((amount, 0), (0, 0), (0, 0)))[:frames]
            taps.append(jnp.einsum('top,tcp->oc', gated, earlier))
            later = jnp.pad(gated, ((0, amount), (0, 0), (0, 0)))[amount:]
            error = error + jnp.einsum('oc,top->tcp', wf[tap], later)
        grads[layer] = jnp.stack(taps)
    return (states[-1], error.astype(jnp.bfloat16), jnp.stack(grads))

def reference(clip, w_space, w_time, cotangent):
    scaling = 1.0 / math.sqrt(FRAMES * H * W)
    activated = lax.map(lambda frame: jax.nn.silu(space_conv(frame, w_space)).astype(jnp.bfloat16), clip)
    u_flat = activated.reshape(FRAMES, C, H * W)
    g_flat = cotangent.reshape(FRAMES, C, H * W)
    cell_count = H * W // N_TILE

    def step(carry, index):
        start = index * cell_count
        u_block = lax.dynamic_slice_in_dim(u_flat, start, cell_count, 2)
        g_block = lax.dynamic_slice_in_dim(g_flat, start, cell_count, 2)
        top, error, grads = time_block(u_block, g_block, w_time)
        return (carry + grads, (top, error))
    init = jnp.zeros((LAYERS, 3, C, C), jnp.float32)
    grad_time, (tops, errors) = lax.scan(step, init, jnp.arange(N_TILE, dtype=jnp.int32))
    output = jnp.transpose(tops, (1, 2, 0, 3)).reshape(FRAMES, C, H, W)
    du = jnp.transpose(errors, (1, 2, 0, 3)).reshape(FRAMES, C, H, W)

    def back_step(carry, pair):
        frame, du_frame = pair
        pre = space_conv(frame, w_space)
        slope_grad = (du_frame.astype(jnp.float32) * silu_slope(pre)).astype(jnp.bfloat16)
        grad_frame, kernel_terms = space_back(frame, slope_grad, w_space)
        return (carry + kernel_terms, grad_frame)
    grad_space, grad_clip = lax.scan(back_step, jnp.zeros((9, C, C), jnp.float32), (clip, du))
    return (output, grad_clip, grad_space * scaling, grad_time * scaling)
```

```python
import math

import jax
import jax.numpy as jnp
from jax import lax
from jax.experimental import pallas as pl
from jax.experimental.pallas import tpu as pltpu
from jax.sharding import PartitionSpec as P

BF16 = jnp.bfloat16
F32 = jnp.float32
CHUNKS = 1
PARAMS = pltpu.CompilerParams(vmem_limit_bytes=56 * 2**20)


def vmem_specs(count):
    return [pl.BlockSpec(memory_space=pltpu.VMEM) for _ in range(count)]


def sigmoid(value):
    return 0.5 * jnp.tanh(0.5 * value) + 0.5


def lane_shifts(left, right):
    lane = lax.broadcasted_iota(jnp.int32, left.shape, 1)
    width = left.shape[1]
    up = jnp.where(lane == 0, 0.0, pltpu.roll(left, 1, 1))
    down = jnp.where(lane == width - 1, 0.0, pltpu.roll(right, width - 1, 1))
    return up, down


def conv_group(source, weights, first, channels, width, flipped):
    operand = jnp.concatenate(
        [
            source[pl.ds(first + 2 * half, 4)].reshape(4 * channels, width)
            for half in range(2)
        ],
        axis=1,
    )
    product = jnp.dot(weights, operand, preferred_element_type=F32)
    rows = []
    for half in range(2):
        for inner in range(2):
            parts = [
                product[
                    (3 * inner + tap) * channels : (3 * inner + tap + 1) * channels,
                    half * width : (half + 1) * width,
                ]
                for tap in range(3)
            ]
            left, right = (parts[2], parts[0]) if flipped else (parts[0], parts[2])
            up, down = lane_shifts(left, right)
            rows.append(parts[1] + up + down)
    return rows


def pack_block(block):
    half = block.shape[0] // 2
    return jnp.concatenate([block[:half], block[half:]], axis=1)


def group_start(group, rows, part, part_rows):
    if part_rows == rows:
        return 4 * group
    per = part_rows // 4
    return (group // per) * rows + part * part_rows + 4 * (group % per)


def space_forward(padded, weights, rows, part, part_rows):
    height, channels, width = padded.shape[0] - 2, padded.shape[1], padded.shape[2]
    count = height * part_rows // rows

    def body(x_ref, w_ref, v_ref, slope_ref):
        @pl.loop(0, count // 4)
        def _(group):
            first = group_start(group, rows, part, part_rows)
            for offset, pre in enumerate(
                conv_group(x_ref, w_ref[...], first, channels, width, False)
            ):
                sigma = sigmoid(pre)
                v_ref[4 * group + offset] = (pre * sigma).astype(BF16)
                slope_ref[4 * group + offset] = sigma * (1.0 + pre * (1.0 - sigma))

    shape = (count, channels, width)
    return pl.pallas_call(
        body,
        out_shape=(jax.ShapeDtypeStruct(shape, BF16), jax.ShapeDtypeStruct(shape, F32)),
        in_specs=vmem_specs(2),
        out_specs=tuple(vmem_specs(2)),
        compiler_params=PARAMS,
        name="space_forward",
    )(padded, weights)


def time_block(v0, cot, fwd, bwd, scaling):
    frames, rows, channels, width = v0.shape
    sets = [(r, r + 1) for r in range(0, rows, 2)] if rows % 2 == 0 else [(r,) for r in range(rows)]

    def side(items):
        return items[0] if len(items) == 1 else jnp.concatenate(items, axis=1)

    def gather(ref, indices, members):
        return side(
            [jnp.concatenate([ref[i, r] for i in indices], axis=0) for r in members]
        )

    def body(v0_ref, cot_ref, fwd_ref, bwd_ref, out_ref, e0_ref, g_ref, v0p, v1p, q0p, q1p, s0, acc):
        empty = jnp.zeros((4, rows, channels, width), BF16)
        v0p[0:4] = empty
        v1p[0:4] = empty
        q0p[frames : frames + 4] = empty
        q1p[frames : frames + 4] = empty
        v0p[4 : frames + 4] = v0_ref[...]
        acc[...] = jnp.zeros(acc.shape, F32)

        def split(value, at, slot):
            return value[at * channels : (at + 1) * channels, slot * width : (slot + 1) * width]

        @pl.loop(0, frames // 4)
        def _(step):
            t0 = 4 * step
            for members in sets:
                for ta in (t0, t0 + 2):
                    mixed = jnp.dot(
                        fwd_ref[0],
                        gather(v0p, [ta + 2 + f for f in range(4)], members),
                        preferred_element_type=F32,
                    )
                    sigma = sigmoid(mixed)
                    gain = mixed * sigma
                    slope = sigma * (1.0 + mixed * (1.0 - sigma))
                    for at in range(2):
                        for slot, r in enumerate(members):
                            now = v0p[ta + at + 4, r].astype(F32)
                            v1p[ta + at + 4, r] = (now + split(gain, at, slot)).astype(BF16)
                            s0[ta + at, r] = split(slope, at, slot)
            for members in sets:
                for ta in (t0, t0 + 1):
                    mixed = jnp.dot(
                        fwd_ref[1],
                        gather(v1p, [ta + 2 * f for f in range(4)], members),
                        preferred_element_type=F32,
                    )
                    sigma = sigmoid(mixed)
                    gain = mixed * sigma
                    slope = sigma * (1.0 + mixed * (1.0 - sigma))
                    for at in range(2):
                        t = ta + 2 * at
                        for slot, r in enumerate(members):
                            now = v1p[t + 4, r].astype(F32)
                            out_ref[t, r] = (now + split(gain, at, slot)).astype(BF16)
                            q1p[t, r] = (cot_ref[t, r].astype(F32) * split(slope, at, slot)).astype(BF16)

        @pl.loop(0, frames // 4)
        def _(step):
            t0 = frames - 4 - 4 * step
            for members in sets:
                e1 = {}
                for ta in (t0, t0 + 1):
                    later = gather(q1p, [ta + 2 * f for f in range(4)], members)
                    back = jnp.dot(bwd_ref[1], later, preferred_element_type=F32)
                    for at in range(2):
                        t = ta + 2 * at
                        for slot, r in enumerate(members):
                            value = cot_ref[t, r].astype(F32) + split(back, at, slot)
                            e1[(0 if ta is t0 else 1) + 2 * at, slot] = value
                            q0p[t, r] = (value * s0[t, r]).astype(BF16)
                    acc[1] += lax.dot_general(
                        later[: 2 * channels],
                        gather(v1p, [ta + 2 * f for f in range(4)], members),
                        (((1,), (1,)), ((), ())),
                        preferred_element_type=F32,
                    )
                for ta, base in ((t0, 0), (t0 + 2, 2)):
                    later = gather(q0p, [ta + f for f in range(4)], members)
                    back = jnp.dot(bwd_ref[0], later, preferred_element_type=F32)
                    for at in range(2):
                        for slot, r in enumerate(members):
                            e0_ref[ta + at, r] = (e1[base + at, slot] + split(back, at, slot)).astype(BF16)
                    acc[0] += lax.dot_general(
                        later[: 2 * channels],
                        gather(v0p, [ta + 2 + f for f in range(4)], members),
                        (((1,), (1,)), ((), ())),
                        preferred_element_type=F32,
                    )

        for layer in range(2):
            for tap in range(3):
                total = sum(
                    acc[
                        layer,
                        at * channels : (at + 1) * channels,
                        (at + 2 - tap) * channels : (at + 3 - tap) * channels,
                    ]
                    for at in range(2)
                )
                index = 3 * layer + tap
                half = channels // 2
                g_ref[index * half : (index + 1) * half] = pack_block(total) * scaling

    shape = (frames, rows, channels, width)
    padded = pltpu.VMEM((frames + 4, rows, channels, width), BF16)
    return pl.pallas_call(
        body,
        out_shape=(
            jax.ShapeDtypeStruct(shape, BF16),
            jax.ShapeDtypeStruct(shape, BF16),
            jax.ShapeDtypeStruct((3 * channels, 2 * channels), F32),
        ),
        in_specs=vmem_specs(4),
        out_specs=tuple(vmem_specs(3)),
        scratch_shapes=[
            padded,
            padded,
            padded,
            padded,
            pltpu.VMEM(shape, F32),
            pltpu.VMEM((2, 2 * channels, 4 * channels), F32),
        ],
        compiler_params=PARAMS,
        name="time_block",
    )(v0, cot, fwd, bwd)


def slope_grad(returned, slopes, padded, rows, part, part_rows, scaling):
    count, channels, width = returned.shape

    def body(du_ref, slope_ref, x_ref, ds_ref, g_ref, acc):
        acc[...] = jnp.zeros(acc.shape, F32)

        @pl.loop(0, count // 4)
        def _(group):
            first = group_start(group, rows, part, part_rows)
            for half in range(2):
                left = []
                right = []
                for inner in range(2):
                    at = 4 * group + 2 * half + inner
                    value = du_ref[at].astype(F32) * slope_ref[at]
                    rounded = value.astype(BF16)
                    ds_ref[at] = rounded
                    value = rounded.astype(F32)
                    up, down = lane_shifts(value, value)
                    left.append(
                        jnp.concatenate([down.astype(BF16), rounded, up.astype(BF16)], axis=0)
                    )
                    right.append(
                        x_ref[pl.ds(first + 2 * half + inner, 3)].reshape(3 * channels, width)
                    )
                acc[...] += lax.dot_general(
                    jnp.concatenate(left, axis=1),
                    jnp.concatenate(right, axis=1),
                    (((1,), (1,)), ((), ())),
                    preferred_element_type=F32,
                )

        half_rows = channels // 2
        for tap_row in range(3):
            for tap_col in range(3):
                index = 3 * tap_row + tap_col
                block = acc[
                    tap_col * channels : (tap_col + 1) * channels,
                    tap_row * channels : (tap_row + 1) * channels,
                ]
                g_ref[index * half_rows : (index + 1) * half_rows] = pack_block(block) * scaling

    return pl.pallas_call(
        body,
        out_shape=(
            jax.ShapeDtypeStruct(returned.shape, BF16),
            jax.ShapeDtypeStruct((9 * channels // 2, 2 * channels), F32),
        ),
        in_specs=vmem_specs(3),
        out_specs=tuple(vmem_specs(2)),
        scratch_shapes=[pltpu.VMEM((3 * channels, 3 * channels), F32)],
        compiler_params=PARAMS,
        name="slope_grad",
    )(returned, slopes, padded)


def space_backward(pieces, weights, rows, height):
    channels, width = pieces[0].shape[1:]
    parts = len(pieces)
    part_rows = rows // parts

    def body(*refs):
        inputs, (w_ref, out_ref, held) = refs[:parts], refs[parts:]
        held[0] = jnp.zeros((channels, width), BF16)
        held[height + 1] = jnp.zeros((channels, width), BF16)
        if parts == 1:
            held[1 : height + 1] = inputs[0][...]
        else:
            for part in range(parts):
                for block in range(height // rows):
                    start = block * rows + part * part_rows
                    held[1 + start : 1 + start + part_rows] = inputs[part][
                        block * part_rows : (block + 1) * part_rows
                    ]

        @pl.loop(0, height // 4)
        def _(group):
            for offset, value in enumerate(
                conv_group(held, w_ref[...], 4 * group, channels, width, True)
            ):
                out_ref[4 * group + offset] = value.astype(BF16)

    return pl.pallas_call(
        body,
        out_shape=jax.ShapeDtypeStruct((height, channels, width), BF16),
        in_specs=vmem_specs(parts + 1),
        out_specs=pl.BlockSpec(memory_space=pltpu.VMEM),
        scratch_shapes=[pltpu.VMEM((height + 2, channels, width), BF16)],
        compiler_params=PARAMS,
        name="space_backward",
    )(*pieces, weights)


def exchange(value):
    return lax.all_to_all(value, "tile", split_axis=0, concat_axis=0, tiled=True)


def total_over_tile(terms):
    devices = lax.axis_size("tile")
    rows, width = terms.shape
    share = -(-rows // devices)
    padded = jnp.pad(terms, ((0, share * devices - rows), (0, 0)))
    mine = exchange(padded.reshape(devices, share, width)).sum(0)
    everyone = exchange(jnp.broadcast_to(mine[None], (devices, share, width)))
    return everyone.reshape(devices * share, width)[:rows]


def unpack(terms, channels):
    taps = terms.shape[0] * 2 // channels
    return (
        terms.reshape(taps, channels // 2, 2, channels)
        .transpose(0, 2, 1, 3)
        .reshape(taps, channels, channels)
    )


def band(blocks, offsets, channels, count_out, count_in):
    rows = []
    zero = jnp.zeros((channels, channels), BF16)
    for i in range(count_out):
        row = [zero] * count_in
        for k, block in enumerate(blocks):
            row[offsets(i, k)] = block
        rows.append(jnp.concatenate(row, axis=1))
    return jnp.concatenate(rows, axis=0)


def per_device(clip, w_space, w_time, cotangent):
    frames, channels, height, width = clip.shape
    devices = lax.axis_size("tile")
    rows = height // devices
    parts = CHUNKS if rows % (4 * CHUNKS) == 0 else 1
    part_rows = rows // parts
    total_frames = frames * devices
    scaling = 1.0 / math.sqrt(total_frames * height * width)

    taps = w_space.reshape(3, 3, channels, channels)
    zero = jnp.zeros((channels, channels), BF16)
    forward_w = jnp.concatenate(
        [
            jnp.concatenate(
                [taps[r - i, b] if 0 <= r - i < 3 else zero for r in range(4)], axis=1
            )
            for i in range(2)
            for b in range(3)
        ],
        axis=0,
    )
    backward_w = jnp.concatenate(
        [
            jnp.concatenate(
                [taps[2 - (r - i), b].T if 0 <= r - i < 3 else zero for r in range(4)], axis=1
            )
            for i in range(2)
            for b in range(3)
        ],
        axis=0,
    )
    time_fwd = jnp.stack(
        [band([w_time[l, k] for k in range(3)], lambda i, k: i + 2 - k, channels, 2, 4) for l in range(2)]
    )
    time_bwd = jnp.stack(
        [band([w_time[l, k].T for k in range(3)], lambda i, k: i + k, channels, 2, 4) for l in range(2)]
    )

    padded = jnp.pad(jnp.transpose(clip[0], (1, 0, 2)), ((1, 1), (0, 0), (0, 0)))
    upstream = jnp.transpose(cotangent, (0, 2, 1, 3))
    slopes = []
    relaid = []
    for part in range(parts):
        v, slope = space_forward(padded, forward_w, rows, part, part_rows)
        slopes.append(slope)
        relaid.append(exchange(v.reshape(devices, part_rows, channels, width)))
    tops = []
    returned = []
    time_terms = 0.0
    for part in range(parts):
        top, error, terms = time_block(
            relaid[part].reshape(total_frames, part_rows, channels, width),
            upstream[:, part * part_rows : (part + 1) * part_rows],
            time_fwd,
            time_bwd,
            scaling,
        )
        tops.append(top)
        time_terms = time_terms + terms
        returned.append(exchange(error).reshape(devices * part_rows, channels, width))
    space_terms = 0.0
    pieces = []
    for part in range(parts):
        ds, terms = slope_grad(returned[part], slopes[part], padded, rows, part, part_rows, scaling)
        pieces.append(ds)
        space_terms = space_terms + terms
    terms = total_over_tile(jnp.concatenate([space_terms, time_terms], axis=0))
    grads = unpack(terms, channels)
    grad_clip = space_backward(pieces, backward_w, rows, height)
    grad_clip = jnp.transpose(grad_clip, (1, 0, 2))[None]
    output = jnp.transpose(jnp.concatenate(tops, axis=1), (0, 2, 1, 3))
    return (output, grad_clip, grads[:9], grads[9:].reshape(w_time.shape))


def solution(mesh):
    return jax.shard_map(
        per_device,
        mesh=mesh,
        in_specs=(P(("run", "tile"), None, None, None), P(), P(), P("run", None, "tile", None)),
        out_specs=(
            P("run", None, "tile", None),
            P(("run", "tile"), None, None, None),
            P("run", None, None),
            P("run", None, None, None),
        ),
        check_vma=False,
    )
```

```python
import math

import jax
import jax.numpy as jnp
from jax import lax
from jax.experimental import pallas as pl
from jax.experimental.pallas import tpu as pltpu
from jax.sharding import PartitionSpec as P


BF16 = jnp.bfloat16
F32 = jnp.float32
CHUNKS = 2


def hbm_specs(count):
    return [pl.BlockSpec(memory_space=pltpu.HBM) for _ in range(count)]


def keep(value):
    return pltpu.with_memory_space_constraint(value, pltpu.HBM)


def grant(mebibytes):
    return pltpu.CompilerParams(vmem_limit_bytes=mebibytes * 2**20)


def vmem_specs(count):
    return [pl.BlockSpec(memory_space=pltpu.VMEM) for _ in range(count)]


def lane_shifts(left, right):
    lane = lax.broadcasted_iota(jnp.int32, left.shape, 1)
    width = left.shape[1]
    up = jnp.where(lane == 0, 0.0, pltpu.roll(left, 1, 1))
    down = jnp.where(lane == width - 1, 0.0, pltpu.roll(right, width - 1, 1))
    return up, down


SLAB = 16


def conv_group(source, weights, first, channels, width, flipped):
    operand = jnp.concatenate(
        [
            source[pl.ds(first + 2 * half, 4)].reshape(4 * channels, width)
            for half in range(2)
        ],
        axis=1,
    )
    product = jnp.dot(weights, operand, preferred_element_type=F32)
    for inner in range(2):
        for slab in range(channels // SLAB):
            base = (inner * (channels // SLAB) + slab) * 3 * SLAB
            for half in range(2):
                parts = [
                    product[
                        base + tap * SLAB : base + (tap + 1) * SLAB,
                        half * width : (half + 1) * width,
                    ]
                    for tap in range(3)
                ]
                left, right = (parts[2], parts[0]) if flipped else (parts[0], parts[2])
                up, down = lane_shifts(left, right)
                yield 2 * half + inner, slice(slab * SLAB, (slab + 1) * SLAB), parts[1] + up + down


def fill_conv(target, blocks, channels):
    zero = jnp.zeros((channels, channels), F32)
    for inner in range(2):
        for tap in range(3):
            band = jnp.concatenate(
                [blocks(r - inner, tap) if 0 <= r - inner < 3 else zero for r in range(4)], axis=1
            ).astype(BF16)
            for slab in range(channels // SLAB):
                base = ((inner * (channels // SLAB) + slab) * 3 + tap) * SLAB
                target[base : base + SLAB] = band[slab * SLAB : (slab + 1) * SLAB]


def fill_forward(target, w_ref, channels):
    fill_conv(target, lambda row, col: 0.5 * w_ref[3 * row + col].astype(F32), channels)


def fill_time(fwd_ref, bwd_ref, time_ref):
    layers, _, channels = time_ref.shape[:3]
    zero = jnp.zeros((channels, channels), F32)
    for layer in range(layers):
        taps = [0.5 * time_ref[layer, k].astype(F32) for k in range(3)]
        turned = [tap.T for tap in taps]
        for i in range(2):
            row = [zero] * 4
            back = [zero] * 4
            for k in range(3):
                row[i + 2 - k] = taps[k]
                back[i + k] = turned[k]
            at = slice(i * channels, (i + 1) * channels)
            fwd_ref[layer, at] = jnp.concatenate(row, axis=1).astype(BF16)
            bwd_ref[layer, at] = jnp.concatenate(back, axis=1).astype(BF16)


def pack_block(block):
    half = block.shape[0] // 2
    return jnp.concatenate([block[:half], block[half:]], axis=1)


def group_start(group, rows, part, part_rows):
    if part_rows == rows:
        return 4 * group
    per = part_rows // 4
    return (group // per) * rows + part * part_rows + 4 * (group % per)


def scratch_rows(height, channels, width):
    return pltpu.VMEM((height + 2, channels, width), BF16)


def clear_edges(held):
    height = held.shape[0] - 2
    empty = jnp.zeros(held.shape[1:], BF16)
    held[0] = empty
    held[height + 1] = empty


def space_forward(clip, weights, index, rows, parts, part, part_rows, pieces, with_slope):
    channels, height, width = clip.shape
    devices = height // rows
    count = devices * part_rows
    shape = (count, channels, width)
    if pieces:
        outs = [jax.ShapeDtypeStruct((part_rows, channels, width), BF16)] * devices
    else:
        outs = [jax.ShapeDtypeStruct(shape, BF16)]
    if with_slope:
        outs += [jax.ShapeDtypeStruct(shape, F32)]
    turned = part == parts - 1
    if turned:
        outs += [jax.ShapeDtypeStruct((height + 2, channels, width), BF16)]
    stages = 4
    stage_rows = height // stages
    streamed = not pieces and part == 0 and part_rows < rows
    share = count // stages
    blocks = stage_rows // rows

    def body(index_ref, x_ref, w_hbm, *refs):
        outputs, refs = refs[: len(outs)], refs[len(outs) :]
        raw, held, matrix, w_ref, v_ref, slope_ref, sems, out_sems = refs
        loads = [
            pltpu.make_async_copy(
                x_ref.at[:, pl.ds(stage * stage_rows, stage_rows)], raw.at[stage], sems.at[stage]
            )
            for stage in range(stages)
        ]
        w_load = pltpu.make_async_copy(w_hbm, w_ref, sems.at[stages])
        w_load.start()
        for load in loads:
            load.start()
        stores = []

        def send(source, target):
            stores.append(pltpu.make_async_copy(source, target, out_sems.at[len(stores)]))
            stores[-1].start()

        clear_edges(held)
        w_load.wait()
        fill_forward(matrix, w_ref, channels)

        def turn_rows(stage):
            loads[stage].wait()

            @pl.loop(0, stage_rows // 16, unroll=2)
            def _(step):
                at = pl.multiple_of(step * 16, 16)
                held[pl.ds(1 + stage * stage_rows + at, 16)] = jnp.swapaxes(
                    raw[stage, :, pl.ds(at, 16), :], 0, 1
                )

        def group(first, v_target, at, slope_at):
            for offset, slab, half in conv_group(held, matrix[...], first, channels, width, False):
                turn = jnp.tanh(half)
                bend = half * turn
                v_target[at + offset, slab] = (half + bend).astype(BF16)
                if with_slope:
                    slope_ref[slope_at + offset, slab] = (1.0 + turn) * ((1.0 + half) - bend)

        if not streamed:
            for stage in range(stages):
                turn_rows(stage)
            if turned:
                send(held, outputs[-1])
        for stage in range(stages):
            if streamed:
                turn_rows(stage)
            if pieces:
                for piece in range(blocks * stage, blocks * (stage + 1)):
                    peer = index_ref[0] ^ piece
                    for inner in range(part_rows // 4):
                        group(
                            peer * rows + part * part_rows + 4 * inner,
                            outputs[piece] if piece else v_ref,
                            4 * inner,
                            peer * part_rows + 4 * inner,
                        )
                if stage == 0:
                    send(v_ref, outputs[0])
                if with_slope:
                    at = pl.ds(((index_ref[0] // blocks) ^ stage) * share, share)
                    send(slope_ref.at[at], outputs[devices].at[at])
            else:

                @pl.loop(stage * share // 4, (stage + 1) * share // 4, unroll=4)
                def _(at):
                    group(group_start(at, rows, part, part_rows), v_ref, 4 * at, 4 * at)

                at = pl.ds(stage * share, share)
                send(v_ref.at[at], outputs[0].at[at])
        for store in stores:
            store.wait()

    kinds = [pltpu.HBM] * len(outs)
    if pieces:
        kinds[1:devices] = [pltpu.VMEM] * (devices - 1)
    outs = [
        pltpu.HBM(out.shape, out.dtype) if kind is pltpu.HBM else out for out, kind in zip(outs, kinds)
    ]
    return pl.pallas_call(
        body,
        out_shape=tuple(outs),
        in_specs=[pl.BlockSpec(memory_space=pltpu.SMEM)] + hbm_specs(2),
        out_specs=tuple(pl.BlockSpec(memory_space=kind) for kind in kinds),
        scratch_shapes=[
            pltpu.VMEM((stages, channels, stage_rows, width), BF16),
            scratch_rows(height, channels, width),
            pltpu.VMEM((6 * channels, 4 * channels), BF16),
            pltpu.VMEM(weights.shape, BF16),
            pltpu.VMEM((part_rows if pieces else count, channels, width), BF16),
            pltpu.VMEM(shape if with_slope else (8, channels, width), F32),
            pltpu.SemaphoreType.DMA((stages + 1,)),
            pltpu.SemaphoreType.DMA((2 * stages + 2,)),
        ],
        compiler_params=grant(20),
        name="space_forward",
    )(index, keep(clip), keep(weights))


def time_block(inputs, cot, natural, w_time, index, part, part_rows, terms, scaling):
    if natural:
        frames, channels, all_rows, width = cot.shape
    else:
        frames, all_rows, channels, width = cot.shape
    rows = part_rows
    count = len(inputs)
    half_rows = channels // 2
    term_rows = 6 * half_rows
    sets = [(r, r + 1) for r in range(0, rows, 2)] if rows % 2 == 0 else [(r,) for r in range(rows)]

    def side(items):
        return items[0] if len(items) == 1 else jnp.concatenate(items, axis=1)

    def gather(ref, indices, members):
        return side(
            [jnp.concatenate([ref[i, r] for i in indices], axis=0) for r in members]
        )

    steps = frames // 4
    whole = (4, channels, all_rows, width) if natural else (4, all_rows, channels, width)

    def body(index_ref, *refs):
        inputs, (cot_hbm, time_ref), refs = refs[:count], refs[count : count + 2], refs[count + 2 :]
        terms_hbm, refs = refs[: len(terms)], refs[len(terms) :]
        top_hbm, packed_hbm, refs = refs[0], refs[1], refs[2:]
        errors, refs = refs[:count], refs[count:]
        v0p, v1p, q0p, q1p, s0, acc, packed, cot_ref, out_ref, e0_ref = refs[:10]
        fwd_ref, bwd_ref, cot_raw, terms_ref = refs[10:14]
        cot_sems, term_sems, in_sems, out_sems, e0_sems = refs[14:]

        def cot_load(step):
            at = pl.ds(4 * step, 4)
            return pltpu.make_async_copy(cot_hbm.at[at], cot_raw.at[at], cot_sems.at[step])

        def top_store(step):
            at = pl.ds(4 * step, 4)
            return pltpu.make_async_copy(out_ref.at[at], top_hbm.at[at], out_sems.at[step])

        def e0_store(step):
            at = pl.ds(4 * step, 4)
            return pltpu.make_async_copy(e0_ref.at[at], errors[0].at[at], e0_sems.at[step])

        loads = []
        if count > 1:
            for piece in range(count):
                target = v0p.at[4 + (index_ref[0] ^ piece)]
                loads.append(pltpu.make_async_copy(inputs[piece], target, in_sems.at[piece]))
        for slot, ref in enumerate(terms_hbm):
            loads.append(pltpu.make_async_copy(ref, terms_ref.at[slot], term_sems.at[slot]))
        for load in loads:
            load.start()

        @pl.loop(0, steps)
        def _(step):
            cot_load(step).start()

        fill_time(fwd_ref, bwd_ref, time_ref)

        empty = jnp.zeros((4, rows, channels, width), BF16)
        v0p[0:4] = empty
        v1p[0:4] = empty
        q0p[frames : frames + 4] = empty
        q1p[frames : frames + 4] = empty
        if count == 1:
            v0p[4 : frames + 4] = inputs[0][...]
        for load in loads:
            load.wait()
        acc[...] = jnp.zeros(acc.shape, F32)

        def split(value, at, slot):
            return value[at * channels : (at + 1) * channels, slot * width : (slot + 1) * width]

        @pl.loop(0, frames // 4, unroll=min(frames // 4, 4))
        def _(step):
            t0 = 4 * step
            cot_load(step).wait()
            for t in range(4):
                if natural:
                    mine = cot_raw[t0 + t, :, part * rows : (part + 1) * rows]
                    cot_ref[t0 + t] = 0.5 * jnp.swapaxes(mine.astype(F32), 0, 1)
                else:
                    cot_ref[t0 + t] = 0.5 * cot_raw[t0 + t, part * rows : (part + 1) * rows].astype(F32)
            for members in sets:
                for ta in (t0, t0 + 2):
                    mixed = jnp.dot(
                        fwd_ref[0],
                        gather(v0p, [ta + 2 + f for f in range(4)], members),
                        preferred_element_type=F32,
                    )
                    turn = jnp.tanh(mixed)
                    bend = mixed * turn
                    gain = mixed + bend
                    slope = (1.0 + turn) * ((1.0 + mixed) - bend)
                    for at in range(2):
                        for slot, r in enumerate(members):
                            now = v0p[ta + at + 4, r].astype(F32)
                            v1p[ta + at + 4, r] = (now + split(gain, at, slot)).astype(BF16)
                            s0[ta + at, r] = split(slope, at, slot)
            for members in sets:
                for ta in (t0, t0 + 1):
                    mixed = jnp.dot(
                        fwd_ref[1],
                        gather(v1p, [ta + 2 * f for f in range(4)], members),
                        preferred_element_type=F32,
                    )
                    turn = jnp.tanh(mixed)
                    bend = mixed * turn
                    gain = mixed + bend
                    slope = (1.0 + turn) * ((1.0 + mixed) - bend)
                    for at in range(2):
                        t = ta + 2 * at
                        for slot, r in enumerate(members):
                            now = v1p[t + 4, r].astype(F32)
                            out_ref[t, r] = (now + split(gain, at, slot)).astype(BF16)
                            q1p[t, r] = (cot_ref[t, r] * split(slope, at, slot)).astype(BF16)
            top_store(step).start()

        @pl.loop(0, frames // 4, unroll=min(frames // 4, 4))
        def _(step):
            t0 = frames - 4 - 4 * step
            lefts = [[], []]
            rights = [[], []]
            for members in sets:
                e1 = {}
                for ta in (t0, t0 + 1):
                    later = gather(q1p, [ta + 2 * f for f in range(4)], members)
                    back = jnp.dot(bwd_ref[1], later, preferred_element_type=F32)
                    for at in range(2):
                        t = ta + 2 * at
                        for slot, r in enumerate(members):
                            value = cot_ref[t, r] + split(back, at, slot)
                            e1[(0 if ta is t0 else 1) + 2 * at, slot] = value
                            q0p[t, r] = (value * s0[t, r]).astype(BF16)
                    lefts[1].append(later[: 2 * channels])
                    rights[1].append(gather(v1p, [ta + 2 * f for f in range(4)], members))
                for ta, base in ((t0, 0), (t0 + 2, 2)):
                    later = gather(q0p, [ta + f for f in range(4)], members)
                    back = jnp.dot(bwd_ref[0], later, preferred_element_type=F32)
                    for at in range(2):
                        for slot, r in enumerate(members):
                            e0_ref[ta + at, r] = (e1[base + at, slot] + split(back, at, slot)).astype(BF16)
                    lefts[0].append(later[: 2 * channels])
                    rights[0].append(gather(v0p, [ta + 2 + f for f in range(4)], members))
            for layer in range(2):
                acc[layer] += lax.dot_general(
                    side(rights[layer]),
                    side(lefts[layer]),
                    (((1,), (1,)), ((), ())),
                    preferred_element_type=F32,
                )
            if count == 1:
                e0_store(steps - 1 - step).start()

        if count > 1:
            mine = pltpu.make_async_copy(e0_ref.at[index_ref[0]], errors[0], e0_sems.at[0])
            mine.start()
            for piece in range(1, count):
                errors[piece][...] = e0_ref[index_ref[0] ^ piece]
        for layer in range(2):
            for tap in range(3):
                total = sum(
                    acc[
                        layer,
                        (at + 2 - tap) * channels : (at + 3 - tap) * channels,
                        at * channels : (at + 1) * channels,
                    ]
                    for at in range(2)
                ).T
                slot = 3 * layer + tap
                piece = pack_block(total) * scaling
                for before in range(len(terms)):
                    piece += terms_ref[before, slot * half_rows : (slot + 1) * half_rows]
                packed[slot * half_rows : (slot + 1) * half_rows] = piece
        done = pltpu.make_async_copy(packed, packed_hbm, in_sems.at[0])
        done.start()
        done.wait()
        if count > 1:
            mine.wait()

        @pl.loop(0, steps)
        def _(step):
            top_store(step).wait()
            if count == 1:
                e0_store(step).wait()

    shape = (frames, rows, channels, width)
    padded = pltpu.VMEM((frames + 4, rows, channels, width), BF16)
    scratch = [
        padded,
        padded,
        padded,
        padded,
        pltpu.VMEM(shape, F32),
        pltpu.VMEM((2, 4 * channels, 2 * channels), F32),
    ]
    scratch += [
        pltpu.VMEM((term_rows, 2 * channels), F32),
        pltpu.VMEM(shape, F32),
        pltpu.VMEM(shape, BF16),
        pltpu.VMEM(shape, BF16),
        pltpu.VMEM((2, 2 * channels, 4 * channels), BF16),
        pltpu.VMEM((2, 2 * channels, 4 * channels), BF16),
        pltpu.VMEM((frames,) + whole[1:], BF16),
        pltpu.VMEM((max(len(terms), 1), term_rows, 2 * channels), F32),
        pltpu.SemaphoreType.DMA((steps,)),
        pltpu.SemaphoreType.DMA((len(terms) + 1,)),
        pltpu.SemaphoreType.DMA((count,)),
        pltpu.SemaphoreType.DMA((steps,)),
        pltpu.SemaphoreType.DMA((steps,)),
    ]
    near = vmem_specs(1)
    if count > 1:
        near = hbm_specs(1) + vmem_specs(count - 1)
        inputs = [keep(inputs[0])] + inputs[1:]
    results = pl.pallas_call(
        body,
        out_shape=(
            pltpu.HBM(shape, BF16),
            pltpu.HBM((term_rows, 2 * channels), F32),
            pltpu.HBM(inputs[0].shape, BF16),
            *(jax.ShapeDtypeStruct(piece.shape, BF16) for piece in inputs[1:]),
        ),
        in_specs=[pl.BlockSpec(memory_space=pltpu.SMEM)]
        + near
        + hbm_specs(1)
        + vmem_specs(1)
        + hbm_specs(len(terms)),
        out_specs=tuple(hbm_specs(3) + vmem_specs(count - 1)),
        scratch_shapes=scratch,
        compiler_params=grant(28 if part_rows < all_rows else 46),
        name="time_block",
    )(index, *inputs, keep(cot), w_time, *map(keep, terms))
    return results[0], [results[1]], list(results[2:])


def emit_output(tops):
    frames, rows, channels, width = tops[0].shape
    parts = len(tops)
    shape = (frames, channels, parts * rows, width)
    steps = 4
    span = frames // steps

    def body(*refs):
        inputs, (out_hbm, held, turned, in_sems, out_sems) = refs[:parts], refs[parts:]
        loads = [
            pltpu.make_async_copy(
                inputs[part].at[pl.ds(step * span, span)],
                held.at[part, pl.ds(step * span, span)],
                in_sems.at[step * parts + part],
            )
            for step in range(steps)
            for part in range(parts)
        ]
        stores = [
            pltpu.make_async_copy(
                turned.at[pl.ds(step * span, span)],
                out_hbm.at[pl.ds(step * span, span)],
                out_sems.at[step],
            )
            for step in range(steps)
        ]
        for load in loads:
            load.start()
        for step in range(steps):
            for load in loads[step * parts : (step + 1) * parts]:
                load.wait()

            @pl.loop(step * span, (step + 1) * span, unroll=True)
            def _(t):
                rows_of = jnp.concatenate([held[part, t] for part in range(parts)], axis=0)
                turned[t] = jnp.swapaxes(rows_of, 0, 1)

            stores[step].start()
        for store in stores:
            store.wait()

    return pl.pallas_call(
        body,
        out_shape=pltpu.HBM(shape, BF16),
        in_specs=hbm_specs(parts),
        out_specs=hbm_specs(1)[0],
        scratch_shapes=[
            pltpu.VMEM((parts,) + tops[0].shape, BF16),
            pltpu.VMEM(shape, BF16),
            pltpu.SemaphoreType.DMA((steps * parts,)),
            pltpu.SemaphoreType.DMA((steps,)),
        ],
        compiler_params=grant(12),
        name="emit_output",
    )(*map(keep, tops))


def slope_grad(returned, slopes, frame, weights, index, earlier, rows, part, part_rows, last, scaling):
    height, channels, width = frame.shape[0] - 2, frame.shape[1], frame.shape[2]
    count = len(returned)
    devices = height // rows
    half_rows = channels // 2
    space_rows = 9 * half_rows
    total_rows = space_rows + (earlier[-1].shape[0] if last else 0)
    source = weights if slopes is None else slopes
    stages = 4
    stage_rows = height // stages
    slope_rows = stage_rows * part_rows // rows
    blocks = stage_rows // rows

    def body(index_ref, *refs):
        inputs, (slope_raw, x_ref), refs = list(refs[:count]), refs[count : count + 2], refs[count + 2 :]
        earlier_refs, refs = refs[: len(earlier)], refs[len(earlier) :]
        ds_ref, packs, refs = refs[0], refs[1:-9], refs[-9:]
        if slopes is None:
            back_ref, packs = packs[-1], packs[:-1]
        acc, packed, held, slope_buf, matrix, own_ref, w_ref, time_ref, sems = refs
        extra = []
        if count > 1:
            extra.append(pltpu.make_async_copy(inputs[0], own_ref, sems.at[2 * stages]))
            inputs[0] = own_ref
        if slopes is None:
            extra.append(pltpu.make_async_copy(slope_raw, w_ref, sems.at[2 * stages + 1]))
        for load in extra:
            load.start()
        if last:
            time_load = pltpu.make_async_copy(earlier_refs[-1], time_ref, sems.at[2 * stages + 2])
            time_load.start()

        def place(stage):
            return stage if count == 1 else (index_ref[0] // blocks) ^ stage

        loads = []
        for stage in range(stages):
            at = place(stage)
            loads.append(
                pltpu.make_async_copy(
                    x_ref.at[pl.ds(at * stage_rows, stage_rows + 2)], held.at[stage], sems.at[stage]
                )
            )
            loads[-1].start()
            if slopes is not None:
                loads.append(
                    pltpu.make_async_copy(
                        slope_raw.at[pl.ds(at * slope_rows, slope_rows)],
                        slope_buf.at[stage],
                        sems.at[stages + stage],
                    )
                )
                loads[-1].start()
        for load in extra:
            load.wait()
        if slopes is None:
            fill_forward(matrix, w_ref, channels)
            fill_conv(
                back_ref, lambda row, col: w_ref[3 * (2 - row) + col].astype(F32).T, channels
            )
        acc[...] = jnp.zeros(acc.shape, F32)

        def group(stage, first, slope_at, du_ref, du_at, at):
            left = []
            right = []
            source = held.at[stage]
            if slopes is None:
                for offset, slab, half in conv_group(
                    source, matrix[...], first, channels, width, False
                ):
                    turn = jnp.tanh(half)
                    slope = (1.0 + turn) * ((1.0 + half) - half * turn)
                    ds_ref[at + offset, slab] = (
                        du_ref[du_at + offset, slab].astype(F32) * slope
                    ).astype(BF16)
            for inner in range(4):
                if slopes is None:
                    rounded = ds_ref[at + inner]
                else:
                    value = du_ref[du_at + inner].astype(F32) * slope_buf[stage, slope_at + inner]
                    rounded = value.astype(BF16)
                    ds_ref[at + inner] = rounded
                value = rounded.astype(F32)
                up, down = lane_shifts(value, value)
                left.append(
                    jnp.concatenate([down.astype(BF16), rounded, up.astype(BF16)], axis=0)
                )
                right.append(source[pl.ds(first + inner, 3)].reshape(3 * channels, width))
            return left, right

        def add(lefts, rights):
            acc[...] += lax.dot_general(
                jnp.concatenate(lefts, axis=1),
                jnp.concatenate(rights, axis=1),
                (((1,), (1,)), ((), ())),
                preferred_element_type=F32,
            )

        per = len(loads) // stages
        for stage in range(stages):
            for load in loads[per * stage : per * (stage + 1)]:
                load.wait()
            if count == 1:

                @pl.loop(0, slope_rows // 4, unroll=min(4, slope_rows // 4))
                def _(step):
                    at = stage * slope_rows + 4 * step
                    add(
                        *group(
                            stage,
                            group_start(step, rows, part, part_rows),
                            4 * step,
                            inputs[0],
                            at,
                            at,
                        )
                    )
            else:
                for piece in range(blocks * stage, blocks * (stage + 1)):
                    local = (index_ref[0] ^ piece) % blocks
                    for inner in range(part_rows // 4):
                        add(
                            *group(
                                stage,
                                local * rows + part * part_rows + 4 * inner,
                                local * part_rows + 4 * inner,
                                inputs[piece],
                                4 * inner,
                                (index_ref[0] ^ piece) * part_rows + 4 * inner,
                            )
                        )

        for tap_row in range(3):
            for tap_col in range(3):
                slot = 3 * tap_row + tap_col
                block = acc[
                    tap_col * channels : (tap_col + 1) * channels,
                    tap_row * channels : (tap_row + 1) * channels,
                ]
                value = pack_block(block) * scaling
                for ref in earlier_refs[: len(earlier) - last]:
                    value += ref[slot * half_rows : (slot + 1) * half_rows]
                packed[slot * half_rows : (slot + 1) * half_rows] = value
        if last:
            time_load.wait()
            packed[space_rows:] = time_ref[...]
            half = total_rows // 2
            own = index_ref[0] % 2
            packs[0][...] = packed[pl.ds(pl.multiple_of(own * half, 8), half)]
            packs[1][...] = packed[pl.ds(pl.multiple_of((1 - own) * half, 8), half)]
        else:
            packs[0][...] = packed[...]

    if last:
        packs = [jax.ShapeDtypeStruct((total_rows // 2, 2 * channels), F32)] * 2
    else:
        packs = [jax.ShapeDtypeStruct((total_rows, 2 * channels), F32)]
    if slopes is None:
        packs = packs + [jax.ShapeDtypeStruct((6 * channels, 4 * channels), BF16)]
    returned = ([keep(returned[0])] if count > 1 else returned[:1]) + returned[1:]
    earlier = earlier[:-1] + [keep(earlier[-1])] if last else earlier
    ds, *packs = pl.pallas_call(
        body,
        out_shape=(jax.ShapeDtypeStruct((devices * part_rows, channels, width), BF16), *packs),
        in_specs=[pl.BlockSpec(memory_space=pltpu.SMEM)]
        + (hbm_specs(1) if count > 1 else vmem_specs(1))
        + vmem_specs(count - 1)
        + hbm_specs(2)
        + vmem_specs(len(earlier) - last)
        + hbm_specs(1 if last else 0),
        out_specs=tuple(vmem_specs(1 + len(packs))),
        scratch_shapes=[
            pltpu.VMEM((3 * channels, 3 * channels), F32),
            pltpu.VMEM((total_rows, 2 * channels), F32),
            pltpu.VMEM((stages, stage_rows + 2, channels, width), BF16),
            pltpu.VMEM((stages, slope_rows, channels, width), F32),
            pltpu.VMEM((6 * channels, 4 * channels), BF16),
            pltpu.VMEM((part_rows, channels, width), BF16),
            pltpu.VMEM(weights.shape, BF16),
            pltpu.VMEM(earlier[-1].shape if last else (8, width), F32),
            pltpu.SemaphoreType.DMA((2 * stages + 3,)),
        ],
        compiler_params=grant(20),
        name="slope_grad",
    )(index, *returned, keep(source), keep(frame), *earlier)
    return ds, packs


def space_backward(pieces, weights, rows, height, first_row, row_count, before):
    channels, width = pieces[0].shape[1:]
    parts = len(pieces)
    part_rows = rows // parts
    shape = (1, channels, height, width)

    low = max(0, first_row // rows - 1)
    high = min(height // rows, -(-(first_row + row_count) // rows) + 1)

    def body(*refs):
        inputs, w_ref = refs[:parts], refs[parts]
        out_ref, held, staged, out_sems, sems = refs[-5:]
        clear_edges(held)
        loads = []
        if parts == 1:
            start, stop = low * rows, high * rows
            loads.append(
                pltpu.make_async_copy(
                    inputs[0].at[pl.ds(start, stop - start)],
                    held.at[pl.ds(1 + start, stop - start)],
                    sems.at[0],
                )
            )
        else:
            for block in range(low, high):
                for part in range(parts):
                    loads.append(
                        pltpu.make_async_copy(
                            inputs[part].at[pl.ds(block * part_rows, part_rows)],
                            held.at[pl.ds(1 + block * rows + part * part_rows, part_rows)],
                            sems.at[len(loads)],
                        )
                    )
        for load in loads:
            load.start()

        def store(group):
            at = pl.multiple_of(8 * group, 8)
            return pltpu.make_async_copy(
                staged.at[:, pl.ds(at, 8)],
                out_ref.at[0, :, pl.ds(pl.multiple_of(first_row + at, 8), 8)],
                out_sems.at[group],
            )

        for load in loads:
            load.wait()

        @pl.loop(0, row_count // 8, unroll=2)
        def _(group):
            grid = [[None] * (channels // SLAB) for _ in range(8)]
            for side in range(2):
                for offset, slab, value in conv_group(
                    held, w_ref[...], first_row + 8 * group + 4 * side, channels, width, True
                ):
                    grid[4 * side + offset][slab.start // SLAB] = value
            block = jnp.stack([jnp.concatenate(row, axis=0) for row in grid])
            staged[:, pl.ds(pl.multiple_of(8 * group, 8), 8), :] = jnp.swapaxes(block, 0, 1).astype(BF16)
            store(group).start()

        @pl.loop(0, row_count // 8)
        def _(group):
            store(group).wait()

    extra = [] if before is None else [keep(before)]
    return pl.pallas_call(
        body,
        out_shape=pltpu.HBM(shape, BF16),
        in_specs=[pl.BlockSpec(memory_space=pl.ANY)] * parts
        + vmem_specs(1)
        + hbm_specs(len(extra)),
        out_specs=pl.BlockSpec(memory_space=pltpu.HBM),
        scratch_shapes=[
            scratch_rows(height, channels, width),
            pltpu.VMEM((channels, row_count, width), BF16),
            pltpu.SemaphoreType.DMA((row_count // 8,)),
            pltpu.SemaphoreType.DMA((parts * (high - low),)),
        ],
        input_output_aliases={parts + 1: 0} if extra else {},
        compiler_params=grant(14),
        name="space_backward",
    )(*pieces, weights, *extra)


def finish(mine, theirs, index, channels):
    half = mine.shape[0]
    taps = 2 * half * 2 // channels

    def body(index_ref, mine_ref, theirs_ref, space_ref, time_ref, joined):
        own = index_ref[0] % 2
        joined[pl.ds(pl.multiple_of(own * half, 8), half)] = mine_ref[...]
        joined[pl.ds(pl.multiple_of((1 - own) * half, 8), half)] = theirs_ref[...]
        for tap in range(taps):
            rows = joined[tap * channels // 2 : (tap + 1) * channels // 2]
            value = jnp.concatenate([rows[:, :channels], rows[:, channels:]], axis=0)
            if tap < 9:
                space_ref[tap] = value
            else:
                time_ref[tap - 9] = value

    return pl.pallas_call(
        body,
        out_shape=(
            jax.ShapeDtypeStruct((9, channels, channels), F32),
            jax.ShapeDtypeStruct((taps - 9, channels, channels), F32),
        ),
        in_specs=[pl.BlockSpec(memory_space=pltpu.SMEM)] + vmem_specs(2),
        out_specs=tuple(vmem_specs(2)),
        scratch_shapes=[pltpu.VMEM((2 * half, 2 * channels), F32)],
        compiler_params=grant(8),
        name="finish",
    )(index, mine, theirs)


def exchange(value):
    return lax.all_to_all(value, "tile", split_axis=0, concat_axis=0, tiled=True)


def swap_pieces(pieces):
    devices = len(pieces)
    return [pieces[0]] + [
        lax.ppermute(pieces[b], "tile", [(i, i ^ b) for i in range(devices)])
        for b in range(1, devices)
    ]


def flip(value, bit):
    devices = lax.axis_size("tile")
    return lax.ppermute(value, "tile", [(i, i ^ bit) for i in range(devices)])


def total_over_tile(mine, other, index, channels, beside):
    devices = lax.axis_size("tile")
    beside = list(beside)
    extra = None
    total = mine + flip(other, 1)
    bit = 2
    while bit < devices:
        received = flip(total, bit)
        if beside and bit != 4:
            extra = beside.pop(0)(extra)
            received, extra = lax.optimization_barrier((received, extra))
        total = total + received
        bit *= 2
    while beside:
        extra = beside.pop(0)(extra)
    return finish(total, flip(total, 1), index, channels), extra


def block(clip, w_space, w_time, cotangent):
    frames, channels, height, width = clip.shape
    devices = lax.axis_size("tile")
    rows = height // devices
    parts = CHUNKS if rows % (4 * CHUNKS) == 0 else 1
    part_rows = rows // parts
    total_frames = frames * devices
    scaling = 1.0 / math.sqrt(total_frames * height * width)

    index = lax.axis_index("tile").astype(jnp.int32).reshape(1)
    natural = rows % 8 == 0
    upstream = cotangent if natural else jnp.transpose(cotangent, (0, 2, 1, 3))
    slopes = []
    relaid = []
    for part in range(parts):
        place = (rows, parts, part, part_rows)
        if part == 0:
            v, *frame = space_forward(clip[0], w_space, index, *place, False, False)
            slopes.append(None)
            relaid.append([exchange(v.reshape(devices, part_rows, channels, width))])
        else:
            *pieces, slope, frame = space_forward(clip[0], w_space, index, *place, True, True)
            slopes.append(slope)
            relaid.append(swap_pieces(pieces))
    if parts == 1:
        (frame,) = frame
    tops = []
    returned = []
    time_terms = []
    for part in range(parts):
        last = part == parts - 1
        top, time_terms, errors = time_block(
            relaid[part],
            upstream,
            natural,
            w_time,
            index,
            part,
            part_rows,
            time_terms,
            scaling,
        )
        if part == 0:
            returned.append([exchange(errors[0]).reshape(devices * part_rows, channels, width)])
        else:
            returned.append(swap_pieces(errors))
        tops.append(top)
    if natural and total_frames % 4 == 0:
        output = emit_output(tops)
    else:
        output = jnp.transpose(jnp.concatenate(tops, axis=1), (0, 2, 1, 3))
    space_terms = []
    pieces = []
    for part in range(parts):
        last = part == parts - 1
        ds, space_terms = slope_grad(
            returned[part],
            slopes[part],
            frame,
            w_space,
            index,
            space_terms + (time_terms if last else []),
            rows,
            part,
            part_rows,
            last,
            scaling,
        )
        pieces.append(ds)
        if part == 0:
            backward_w = space_terms.pop()
    edges = [0, 56, 128]
    edges = [edge * height // 128 for edge in edges]
    beside = [
        lambda before, start=start, stop=stop: space_backward(
            pieces, backward_w, rows, height, start, stop - start, before
        )
        for start, stop in zip(edges[:-1], edges[1:])
    ]
    (grad_space, grad_time), grad_clip = total_over_tile(*space_terms, index, channels, beside)
    return (output, grad_clip, grad_space, grad_time.reshape(w_time.shape))


def solution(mesh):
    return jax.shard_map(
        block,
        mesh=mesh,
        in_specs=(P(("run", "tile"), None, None, None), P(), P(), P("run", None, "tile", None)),
        out_specs=(
            P("run", None, "tile", None),
            P(("run", "tile"), None, None, None),
            P("run", None, None),
            P("run", None, None, None),
        ),
        check_vma=False,
    )
```
